32 devices in a mesh: grp: 2 (over y), seg: 16 (over z, x, core).
Axes of the slice: x: 2, y: 2, z: 4, core: 2. Of those that a mesh axis runs over, the one named last changes fastest.
Arguments:
- strain: bfloat16 [524288], P(('grp', 'seg')), parts along dimension 0, may hold values from -6 to 6
- templates: bfloat16 [128, 512], P('seg'), may hold values from -6 to 6
Outputs:
- profile: float32 [32, 128], P(('grp', 'seg')), parts along dimension 0
- overall: float32 [256], P('grp'), parts along dimension 0
The draws below stay inside these ranges and needn't reach their ends.
There are 2 independent parts, one for each index of `grp`. The reference program is written for one: setup_inputs(seed, part) draws one part's arguments, and reference() takes and returns one part's arrays. A program takes and returns all parts, laid end to end along the dimension named above; an argument that names none is the same for every part. Nothing has to cross between parts.
All inputs are finite; a program needn't handle non-finite values.
Results may differ from the reference program's by a relative error of at most 0.0003.
Values may be sent and summed in bfloat16 or wider, within the bound.
A program may use at most 256 MiB of HBM per device.

```python
import jax
import jax.numpy as jnp
from jax import lax

QUERIES = 128
M = 512
SEG_LEN = 16384
SAMPLES = 262144
N_SEG = 16


def block_levels(rng, extent, cuts, low, high):
    def one(position, shards_of):
        draws = jax.random.uniform(jax.random.fold_in(jax.random.fold_in(rng, 6), position), (shards_of,), jnp.float32, low / len(cuts), high / len(cuts))
        return jnp.repeat(jnp.exp(draws), extent[position] // shards_of).reshape((-1,) + (1,) * (len(extent) - position - 1))

    level = one(*cuts[0])
    for cut in cuts[1:]:
        level = level * one(*cut)
    return level


def centred(stream_key, extent, deviation, bound, pieces=(), kind=jnp.bfloat16):
    level = block_levels(stream_key, extent, pieces, -0.22, 0.18) if pieces else 1.0
    drawn = jax.random.normal(stream_key, extent, jnp.float32) * deviation * level
    return jnp.minimum(jnp.maximum(drawn, -bound), bound).astype(kind)


def setup_inputs(seed: int = 0, part: int = 0) -> dict:
    streams_of = jax.random.split(jax.random.key(seed), 3)
    part_keys = jax.random.split(jax.random.fold_in(streams_of[2], part), 3)
    strain = centred(part_keys[0], (SAMPLES,), 1.0, 6.0, ((0, 16),))
    templates = centred(streams_of[1], (QUERIES, M), 1.0, 6.0, ((0, 16),))
    return {"strain": strain, "templates": templates}


EPSILON = 1e-05

def hankel(extended, width):
    count = (extended.shape[0] - width) // width
    lower = extended[:count * width].reshape(count, width)
    upper = extended[width:].reshape(count, width)
    paired = jnp.concatenate([lower, upper], axis=1)
    tiled = jnp.tile(paired, (1, width + 1))[:, :width * (2 * width + 1)]
    windows = tiled.reshape(count, width, 2 * width + 1)[:, :, :width].reshape(count * width, width)
    return (paired, windows)

def window_stats(paired, width):
    rows = jnp.arange(2 * width)[:, None]
    cols = jnp.arange(width)[None, :]
    ones_band = ((rows >= cols) & (rows < cols + width)).astype(jnp.float32)
    floats = paired.astype(jnp.float32)
    totals = jnp.dot(floats, ones_band, precision=lax.Precision.HIGHEST).reshape(-1)
    squared = jnp.dot(floats * floats, ones_band, precision=lax.Precision.HIGHEST).reshape(-1)
    win_mean = totals / width
    variance = squared / width - win_mean * win_mean
    return (win_mean, jnp.sqrt(jnp.maximum(variance, 0.0) + EPSILON))

def template_minima(windows, win_mean, win_dev, usable, templates):
    width = templates.shape[1]
    floats = templates.astype(jnp.float32)
    t_mean = lax.optimization_barrier(jnp.mean(floats, axis=1))
    t_dev = jnp.sqrt(lax.optimization_barrier(jnp.mean((floats - t_mean[:, None]) ** 2, axis=1)) + EPSILON)
    products = lax.dot_general(windows, templates, (((1,), (1,)), ((), ())), preferred_element_type=jnp.float32)
    rho = (products - width * win_mean[:, None] * t_mean[None, :]) / (width * win_dev[:, None] * t_dev[None, :])
    distance = jnp.sqrt(jnp.maximum(2.0 - 2.0 * rho, 0.0))
    distance = jnp.where(usable[:, None], distance, jnp.inf)
    return lax.optimization_barrier(jnp.min(distance, axis=0))

def reference(strain, templates):
    padded = jnp.concatenate([strain, jnp.zeros((M,), jnp.bfloat16)])

    def segment(number):
        extended = lax.dynamic_slice_in_dim(padded, number * SEG_LEN, SEG_LEN + M)
        paired, windows = hankel(extended, M)
        win_mean, win_dev = window_stats(paired, M)
        places = number * SEG_LEN + jnp.arange(SEG_LEN, dtype=jnp.int32)
        usable = places <= SEG_LEN * N_SEG - M
        return template_minima(windows, win_mean, win_dev, usable, templates)
    profile = lax.map(segment, jnp.arange(N_SEG, dtype=jnp.int32))
    return (profile, lax.optimization_barrier(jnp.min(profile, axis=0)))
```

```python
import functools

import jax
import jax.numpy as jnp
from jax import lax
from jax.experimental import pallas as pl
from jax.experimental.pallas import tpu as pltpu
from jax.sharding import PartitionSpec as P

EPSILON = 1e-05
LANES = 128
SUBLANES = 8
PACKED = 16
MESH = pl.DeviceIdType.MESH


def each(count, body):
    if count <= 16:
        for step in range(count):
            body(step)
    else:
        lax.fori_loop(0, count, lambda step, _: (body(step), 0)[1], 0)


def largest_divisor(number, bound):
    return max(d for d in range(1, bound + 1) if number % d == 0)


def later(rows, samples):
    turned = pltpu.roll(rows, LANES - samples, 1)
    below = jnp.concatenate([turned[1:], turned[:1]], axis=0)
    lane = lax.broadcasted_iota(jnp.int32, rows.shape, 1)
    return jnp.where(lane < LANES - samples, turned, below)


def window_sums(rows, width):
    span = 1
    while span < LANES:
        rows = rows + later(rows, span)
        span *= 2
    while span < width:
        step = span // LANES
        rows = rows + jnp.concatenate([rows[step:], rows[:step]], axis=0)
        span *= 2
    return rows


def kernel(n, width, gathers, strain_ref, templates_ref, profile_ref, overall_ref,
           halo, gathered, near, hankel, sums, scales, minima, mine,
           halo_send, halo_recv, send, recv, out_send, out_recv):
    me = lax.axis_index("seg")
    grp = lax.axis_index("grp")
    rows = strain_ref.shape[0]
    extra = width // LANES
    tiles = rows + extra
    padded = near.shape[1] // LANES
    before = lax.rem(me + n - 1, n)

    def peer(step):
        return lax.rem(me + step + 1, n)

    barrier = pltpu.get_barrier_semaphore()
    each(n - 1, lambda step: pl.semaphore_signal(
        barrier, inc=1, device_id=(grp, peer(step)), device_id_type=MESH))

    def spread(values, first, count):
        for row in range(count):
            near[:, pl.ds((first + row) * LANES, LANES)] = jnp.broadcast_to(
                values[row : row + 1], (SUBLANES, LANES))

    def stagger(start, count):
        span = (count + 1) * LANES
        sub = lax.broadcasted_iota(jnp.int32, (SUBLANES, span), 0)
        base = near[:, pl.ds(start, span)]
        for bit in (1, 2, 4):
            base = jnp.where((sub & bit) != 0, pltpu.roll(base, span - bit, 1), base)
        for pair in range(LANES // PACKED):
            both = []
            for half in range(2):
                amount = pair * PACKED + half * SUBLANES
                turned = base if amount == 0 else pltpu.roll(base, span - amount, 1)
                both.append(turned[:, : count * LANES])
            hankel[pl.ds(pair * PACKED, PACKED), pl.ds(start, count * LANES)] = (
                jnp.concatenate(both, axis=0).astype(jnp.bfloat16))

    strain = strain_ref[...].astype(jnp.float32)
    spread(strain, 0, rows)
    early = rows - SUBLANES
    chunk = largest_divisor(early, 10)

    def build(step, _):
        stagger(pl.multiple_of(step * (chunk * LANES), LANES), chunk)
        return 0

    lax.fori_loop(0, early // chunk, build, 0)

    pl.semaphore_wait(barrier, n - 1)

    halo_copy = pltpu.make_async_remote_copy(
        src_ref=strain_ref.at[pl.ds(0, PACKED)], dst_ref=halo,
        send_sem=halo_send, recv_sem=halo_recv, device_id=(grp, before), device_id_type=MESH)
    halo_copy.start()

    def template_copy(step):
        return pltpu.make_async_remote_copy(
            src_ref=templates_ref, dst_ref=gathered.at[me],
            send_sem=send.at[step], recv_sem=recv.at[step],
            device_id=(grp, peer(step)), device_id_type=MESH)

    if gathers:
        each(n - 1, lambda step: template_copy(step).start())
        gathered[me] = templates_ref[...]

    halo_copy.wait()
    following = halo[...].astype(jnp.float32)
    following = jnp.where(me == n - 1, jnp.zeros_like(following), following)
    spread(following, rows, padded - rows)
    stagger(early * LANES, tiles - early)

    extended = jnp.concatenate([strain, following[:SUBLANES]], axis=0)
    totals = window_sums(extended, width)[:rows]
    squared = window_sums(extended * extended, width)[:rows]
    win_mean = totals / width
    win_dev = jnp.sqrt(jnp.maximum(squared / width - win_mean * win_mean, 0.0) + EPSILON)
    sums[...] = totals
    scales[...] = 1.0 / win_dev

    if gathers:
        each(n - 1, lambda step: template_copy(step).wait())
        floats = gathered[...].astype(jnp.float32).reshape(-1, width)
    else:
        floats = templates_ref[...].astype(jnp.float32)
    templates = floats.astype(jnp.bfloat16)
    queries = floats.shape[0]
    t_mean = jnp.mean(floats, axis=1, keepdims=True)
    t_dev = jnp.sqrt(jnp.mean((floats - t_mean) ** 2, axis=1, keepdims=True) + EPSILON)
    t_wide = jnp.broadcast_to(t_mean, (queries, LANES))

    def scores(tile, count):
        block = jnp.concatenate(
            [hankel[:, pl.ds(pl.multiple_of((tile + c) * LANES, LANES), count * LANES)]
             for c in range(extra)], axis=0)
        products = jnp.dot(templates, block, preferred_element_type=jnp.float32)
        return [
            (products[:, h * LANES : (h + 1) * LANES] - sums[pl.ds(tile + h, 1), :] * t_wide)
            * scales[pl.ds(tile + h, 1), :]
            for h in range(count)
        ]

    pairs = (rows - extra) // 2

    def fold(step, best):
        one, two = scores(step * 2, 2)
        return jnp.maximum(best, jnp.maximum(one, two))

    best = lax.fori_loop(0, pairs, fold, jnp.full((queries, LANES), -jnp.inf, jnp.float32))
    lane = lax.broadcasted_iota(jnp.int32, (1, LANES), 1)
    for tile in range(2 * pairs, rows, 2):
        for h, score in enumerate(scores(tile, 2)):
            last = (tile + h) * LANES + lane
            usable = (me < n - 1) | (last <= rows * LANES - width)
            best = jnp.maximum(best, jnp.where(usable, score, -jnp.inf))
    best = best / (width * t_dev)
    rho = jnp.max(best.T, axis=0, keepdims=True)
    distance = jnp.sqrt(jnp.maximum(2.0 - 2.0 * rho, 0.0))
    profile_ref[...] = distance
    mine[...] = distance
    minima[me] = distance

    def out_copy(step):
        return pltpu.make_async_remote_copy(
            src_ref=mine, dst_ref=minima.at[me],
            send_sem=out_send.at[step], recv_sem=out_recv.at[step],
            device_id=(grp, peer(step)), device_id_type=MESH)

    each(n - 1, lambda step: out_copy(step).start())
    each(n - 1, lambda step: out_copy(step).wait())
    overall_ref[...] = jnp.min(minima[...], axis=0)


def per_device(n, strain, templates):
    width = templates.shape[1]
    held = templates.shape[0]
    queries = n * held
    gathers = held % SUBLANES == 0
    if not gathers:
        templates = lax.all_gather(templates, "seg", axis=0, tiled=True)
    rows = strain.shape[0] // LANES
    extra = width // LANES
    padded = rows + SUBLANES
    dma = pltpu.SemaphoreType.DMA
    vmem = pl.BlockSpec(memory_space=pltpu.VMEM)
    profile, overall = pl.pallas_call(
        functools.partial(kernel, n, width, gathers),
        out_shape=[jax.ShapeDtypeStruct((1, queries), jnp.float32)] * 2,
        in_specs=[vmem] * 2,
        out_specs=[vmem] * 2,
        scratch_shapes=[
            pltpu.VMEM((PACKED, LANES), jnp.bfloat16),
            pltpu.VMEM((n, max(held, SUBLANES), width), jnp.bfloat16),
            pltpu.VMEM((SUBLANES, padded * LANES), jnp.float32),
            pltpu.VMEM((LANES, (rows + extra) * LANES), jnp.bfloat16),
            pltpu.VMEM((rows, LANES), jnp.float32),
            pltpu.VMEM((rows, LANES), jnp.float32),
            pltpu.VMEM((n, 1, queries), jnp.float32),
            pltpu.VMEM((1, queries), jnp.float32),
            dma, dma, dma((n - 1,)), dma((n - 1,)), dma((n - 1,)), dma((n - 1,)),
        ],
        compiler_params=pltpu.CompilerParams(collective_id=0, has_side_effects=True),
    )(strain.reshape(rows, LANES), templates)
    return (profile, overall.reshape(-1))


def solution(mesh):
    in_specs = (P(("grp", "seg")), P("seg", None))
    out_specs = (P(("grp", "seg"), None), P("grp"))
    return jax.shard_map(
        functools.partial(per_device, mesh.shape["seg"]),
        mesh=mesh, in_specs=in_specs, out_specs=out_specs, check_vma=False,
    )
```

```python
import functools

import jax
import jax.numpy as jnp
from jax import lax
from jax.experimental import pallas as pl
from jax.experimental.pallas import tpu as pltpu
from jax.sharding import PartitionSpec as P

EPSILON = 1e-05
LANES = 128
SUBLANES = 8
PACKED = 16
BATCH = 40
GROUP = 4
MESH = pl.DeviceIdType.MESH


def each(count, body):
    if count <= 16:
        for step in range(count):
            body(step)
    else:
        lax.fori_loop(0, count, lambda step, _: (body(step), 0)[1], 0)


def largest_divisor(number, bound):
    return max(d for d in range(1, bound + 1) if number % d == 0)


def later(rows, samples):
    turned = pltpu.roll(rows, LANES - samples, 1)
    below = jnp.concatenate([turned[1:], turned[:1]], axis=0)
    lane = lax.broadcasted_iota(jnp.int32, rows.shape, 1)
    return jnp.where(lane < LANES - samples, turned, below)


def largest_multiple(number, of):
    return number // of * of


def window_sums(rows, width):
    span = 1
    while span < LANES:
        rows = rows + later(rows, span)
        span *= 2
    while span < width:
        step = span // LANES
        rows = rows + jnp.concatenate([rows[step:], rows[:step]], axis=0)
        span *= 2
    return rows


def kernel(n, width, gathers, strain_ref, templates_ref, profile_ref, overall_ref,
           halo, gathered, near, hankel, sums, scales, minima, mine,
           halo_send, halo_recv, send, recv, out_send, out_recv):
    me = lax.axis_index("seg")
    grp = lax.axis_index("grp")
    rows = strain_ref.shape[0]
    extra = width // LANES
    tiles = rows + extra
    padded = near.shape[1] // LANES
    before = lax.rem(me + n - 1, n)

    def peer(step):
        return lax.rem(me + step + 1, n)

    barrier = pltpu.get_barrier_semaphore()
    each(n - 1, lambda step: pl.semaphore_signal(
        barrier, inc=1, device_id=(grp, peer(step)), device_id_type=MESH))

    def spread(values, first, count):
        for row in range(count):
            near[:, pl.ds((first + row) * LANES, LANES)] = jnp.broadcast_to(
                values[row : row + 1], (SUBLANES, LANES))

    def stagger(start, count):
        span = (count + 1) * LANES
        sub = lax.broadcasted_iota(jnp.int32, (SUBLANES, span), 0)
        base = near[:, pl.ds(start, span)]
        for bit in (1, 2, 4):
            base = jnp.where((sub & bit) != 0, pltpu.roll(base, span - bit, 1), base)
        for pair in range(LANES // PACKED):
            both = []
            for half in range(2):
                amount = pair * PACKED + half * SUBLANES
                turned = base if amount == 0 else pltpu.roll(base, span - amount, 1)
                both.append(turned[:, : count * LANES])
            hankel[pl.ds(pair * PACKED, PACKED), pl.ds(start, count * LANES)] = (
                jnp.concatenate(both, axis=0).astype(jnp.bfloat16))

    strain = strain_ref[...].astype(jnp.float32)
    spread(strain, 0, rows)
    early = rows - SUBLANES
    chunk = largest_divisor(early, 10)

    def build(step, _):
        stagger(pl.multiple_of(step * (chunk * LANES), LANES), chunk)
        return 0

    lax.fori_loop(0, early // chunk, build, 0)

    pl.semaphore_wait(barrier, n - 1)

    halo_copy = pltpu.make_async_remote_copy(
        src_ref=strain_ref.at[pl.ds(0, PACKED)], dst_ref=halo,
        send_sem=halo_send, recv_sem=halo_recv, device_id=(grp, before), device_id_type=MESH)
    halo_copy.start()

    def template_copy(step):
        return pltpu.make_async_remote_copy(
            src_ref=templates_ref, dst_ref=gathered.at[me],
            send_sem=send.at[step], recv_sem=recv.at[step],
            device_id=(grp, peer(step)), device_id_type=MESH)

    if gathers:
        each(n - 1, lambda step: template_copy(step).start())
        gathered[me] = templates_ref[...]

    halo_copy.wait()
    following = halo[...].astype(jnp.float32)
    following = jnp.where(me == n - 1, jnp.zeros_like(following), following)
    spread(following, rows, padded - rows)
    stagger(early * LANES, tiles - early)

    extended = jnp.concatenate([strain, following[:SUBLANES]], axis=0)
    totals = window_sums(extended, width)[:rows]
    squared = window_sums(extended * extended, width)[:rows]
    win_mean = totals / width
    win_dev = jnp.sqrt(jnp.maximum(squared / width - win_mean * win_mean, 0.0) + EPSILON)
    sums[...] = totals
    scales[...] = 1.0 / win_dev

    if gathers:
        each(n - 1, lambda step: template_copy(step).wait())
        floats = gathered[...].astype(jnp.float32).reshape(-1, width)
    else:
        floats = templates_ref[...].astype(jnp.float32)
    templates = floats.astype(jnp.bfloat16)
    queries = floats.shape[0]
    t_mean = jnp.mean(floats, axis=1, keepdims=True)
    t_dev = jnp.sqrt(jnp.mean((floats - t_mean) ** 2, axis=1, keepdims=True) + EPSILON)
    t_wide = jnp.broadcast_to(t_mean, (queries, LANES))

    def scores(tile, count):
        block = jnp.concatenate(
            [hankel[:, pl.ds(pl.multiple_of((tile + c) * LANES, LANES), count * LANES)]
             for c in range(extra)], axis=0)
        products = jnp.dot(templates, block, preferred_element_type=jnp.float32)
        return [
            (products[:, h * LANES : (h + 1) * LANES] - sums[pl.ds(tile + h, 1), :] * t_wide)
            * scales[pl.ds(tile + h, 1), :]
            for h in range(count)
        ]

    def fold(start, count, best):
        for score in scores(start, count):
            best = jnp.maximum(best, score)
        return best

    main = largest_multiple(rows - extra, BATCH)

    def batch(step, best):
        for part in range(BATCH // GROUP):
            best = fold(step * BATCH + part * GROUP, GROUP, best)
        return best

    best = lax.fori_loop(
        0, main // BATCH, batch, jnp.full((queries, LANES), -jnp.inf, jnp.float32))
    lane = lax.broadcasted_iota(jnp.int32, (1, LANES), 1)
    for tile in range(main, rows, 2):
        for h, score in enumerate(scores(tile, 2)):
            if tile + h >= rows - extra:
                last = (tile + h) * LANES + lane
                usable = (me < n - 1) | (last <= rows * LANES - width)
                score = jnp.where(usable, score, -jnp.inf)
            best = jnp.maximum(best, score)
    best = best / (width * t_dev)
    rho = jnp.max(best.T, axis=0, keepdims=True)
    distance = jnp.sqrt(jnp.maximum(2.0 - 2.0 * rho, 0.0))
    profile_ref[...] = distance
    mine[...] = distance
    minima[me] = distance

    def out_copy(step):
        return pltpu.make_async_remote_copy(
            src_ref=mine, dst_ref=minima.at[me],
            send_sem=out_send.at[step], recv_sem=out_recv.at[step],
            device_id=(grp, peer(step)), device_id_type=MESH)

    each(n - 1, lambda step: out_copy(step).start())
    each(n - 1, lambda step: out_copy(step).wait())
    overall_ref[...] = jnp.min(minima[...], axis=0)


def per_device(n, strain, templates):
    width = templates.shape[1]
    held = templates.shape[0]
    queries = n * held
    gathers = held % SUBLANES == 0
    if not gathers:
        templates = lax.all_gather(templates, "seg", axis=0, tiled=True)
    rows = strain.shape[0] // LANES
    extra = width // LANES
    padded = rows + SUBLANES
    dma = pltpu.SemaphoreType.DMA
    vmem = pl.BlockSpec(memory_space=pltpu.VMEM)
    profile, overall = pl.pallas_call(
        functools.partial(kernel, n, width, gathers),
        out_shape=[jax.ShapeDtypeStruct((1, queries), jnp.float32)] * 2,
        in_specs=[vmem] * 2,
        out_specs=[vmem] * 2,
        scratch_shapes=[
            pltpu.VMEM((PACKED, LANES), jnp.bfloat16),
            pltpu.VMEM((n, max(held, SUBLANES), width), jnp.bfloat16),
            pltpu.VMEM((SUBLANES, padded * LANES), jnp.float32),
            pltpu.VMEM((LANES, (rows + extra) * LANES), jnp.bfloat16),
            pltpu.VMEM((rows, LANES), jnp.float32),
            pltpu.VMEM((rows, LANES), jnp.float32),
            pltpu.VMEM((n, 1, queries), jnp.float32),
            pltpu.VMEM((1, queries), jnp.float32),
            dma, dma, dma((n - 1,)), dma((n - 1,)), dma((n - 1,)), dma((n - 1,)),
        ],
        compiler_params=pltpu.CompilerParams(collective_id=0, has_side_effects=True),
    )(strain.reshape(rows, LANES), templates)
    return (profile, overall.reshape(-1))


def solution(mesh):
    in_specs = (P(("grp", "seg")), P("seg", None))
    out_specs = (P(("grp", "seg"), None), P("grp"))
    return jax.shard_map(
        functools.partial(per_device, mesh.shape["seg"]),
        mesh=mesh, in_specs=in_specs, out_specs=out_specs, check_vma=False,
    )
```

```python
import functools

import jax
import jax.numpy as jnp
from jax import lax
from jax.experimental import pallas as pl
from jax.experimental.pallas import tpu as pltpu
from jax.sharding import PartitionSpec as P

EPSILON = 1e-05
LANES = 128
SUBLANES = 8
PACKED = 16
BATCH = 40
GROUP = 4
AHEAD = 3
MESH = pl.DeviceIdType.MESH


def each(count, body):
    if count <= 16:
        for step in range(count):
            body(step)
    else:
        lax.fori_loop(0, count, lambda step, _: (body(step), 0)[1], 0)


def largest_divisor(number, bound):
    return max(d for d in range(1, bound + 1) if number % d == 0)


def later(rows, samples):
    turned = pltpu.roll(rows, LANES - samples, 1)
    below = jnp.concatenate([turned[1:], turned[:1]], axis=0)
    lane = lax.broadcasted_iota(jnp.int32, rows.shape, 1)
    return jnp.where(lane < LANES - samples, turned, below)


def largest_multiple(number, of):
    return number // of * of


def window_sums(rows, width):
    span = 1
    while span < LANES:
        rows = rows + later(rows, span)
        span *= 2
    while span < width:
        step = span // LANES
        rows = rows + jnp.concatenate([rows[step:], rows[:step]], axis=0)
        span *= 2
    return rows


def kernel(n, width, gathers, strain_any, templates_any, profile_ref, overall_ref,
           strain_ref, templates_ref, halo, gathered, near, hankel, sums, scales, minima, mine,
           local, halo_send, halo_recv, send, recv, out_send, out_recv):
    me = lax.axis_index("seg")
    grp = lax.axis_index("grp")
    rows = strain_ref.shape[0]
    extra = width // LANES
    tiles = rows + extra
    padded = near.shape[1] // LANES
    before = lax.rem(me + n - 1, n)

    def peer(step):
        return lax.rem(me + step + 1, n)

    fetches = [
        pltpu.make_async_copy(strain_any, strain_ref, local.at[0]),
        pltpu.make_async_copy(templates_any, templates_ref, local.at[1]),
    ]
    for fetch in fetches:
        fetch.start()
    barrier = pltpu.get_barrier_semaphore()
    each(n - 1, lambda step: pl.semaphore_signal(
        barrier, inc=1, device_id=(grp, peer(step)), device_id_type=MESH))

    def spread(values, first, count):
        for row in range(count):
            near[:, pl.ds((first + row) * LANES, LANES)] = jnp.broadcast_to(
                values[row : row + 1], (SUBLANES, LANES))

    def stagger(start, count):
        span = (count + 1) * LANES
        sub = lax.broadcasted_iota(jnp.int32, (SUBLANES, span), 0)
        base = near[:, pl.ds(start, span)]
        for bit in (1, 2, 4):
            base = jnp.where((sub & bit) != 0, pltpu.roll(base, span - bit, 1), base)
        for pair in range(LANES // PACKED):
            both = []
            for half in range(2):
                amount = pair * PACKED + half * SUBLANES
                turned = base if amount == 0 else pltpu.roll(base, span - amount, 1)
                both.append(turned[:, : count * LANES])
            hankel[pl.ds(pair * PACKED, PACKED), pl.ds(start, count * LANES)] = (
                jnp.concatenate(both, axis=0).astype(jnp.bfloat16))

    for fetch in fetches:
        fetch.wait()
    strain = strain_ref[...].astype(jnp.float32)
    spread(strain, 0, rows)
    early = rows - SUBLANES
    chunk = largest_divisor(early, 10)

    def build(step, _):
        stagger(pl.multiple_of(step * (chunk * LANES), LANES), chunk)
        return 0

    steps = early // chunk
    ahead = steps // AHEAD
    lax.fori_loop(0, ahead, build, 0)

    pl.semaphore_wait(barrier, n - 1)

    halo_copy = pltpu.make_async_remote_copy(
        src_ref=strain_ref.at[pl.ds(0, PACKED)], dst_ref=halo,
        send_sem=halo_send, recv_sem=halo_recv, device_id=(grp, before), device_id_type=MESH)
    halo_copy.start()

    def template_copy(step):
        return pltpu.make_async_remote_copy(
            src_ref=templates_ref, dst_ref=gathered.at[me],
            send_sem=send.at[step], recv_sem=recv.at[step],
            device_id=(grp, peer(step)), device_id_type=MESH)

    if gathers:
        each(n - 1, lambda step: template_copy(step).start())
        gathered[me] = templates_ref[...]

    lax.fori_loop(ahead, steps, build, 0)
    halo_copy.wait()
    following = halo[...].astype(jnp.float32)
    following = jnp.where(me == n - 1, jnp.zeros_like(following), following)
    spread(following, rows, padded - rows)
    stagger(early * LANES, tiles - early)

    extended = jnp.concatenate([strain, following[:SUBLANES]], axis=0)
    totals = window_sums(extended, width)[:rows]
    squared = window_sums(extended * extended, width)[:rows]
    win_mean = totals / width
    win_dev = jnp.sqrt(jnp.maximum(squared / width - win_mean * win_mean, 0.0) + EPSILON)
    sums[...] = totals
    scales[...] = 1.0 / win_dev

    if gathers:
        each(n - 1, lambda step: template_copy(step).wait())
        floats = gathered[...].astype(jnp.float32).reshape(-1, width)
    else:
        floats = templates_ref[...].astype(jnp.float32)
    templates = floats.astype(jnp.bfloat16)
    queries = floats.shape[0]
    t_mean = jnp.mean(floats, axis=1, keepdims=True)
    t_dev = jnp.sqrt(jnp.mean((floats - t_mean) ** 2, axis=1, keepdims=True) + EPSILON)
    t_wide = jnp.broadcast_to(t_mean, (queries, LANES))

    def scores(tile, count):
        block = jnp.concatenate(
            [hankel[:, pl.ds(pl.multiple_of((tile + c) * LANES, LANES), count * LANES)]
             for c in range(extra)], axis=0)
        products = jnp.dot(templates, block, preferred_element_type=jnp.float32)
        return [
            (products[:, h * LANES : (h + 1) * LANES] - sums[pl.ds(tile + h, 1), :] * t_wide)
            * scales[pl.ds(tile + h, 1), :]
            for h in range(count)
        ]

    def fold(start, count, best):
        for score in scores(start, count):
            best = jnp.maximum(best, score)
        return best

    main = largest_multiple(rows - extra, BATCH)

    def batch(step, best):
        for part in range(BATCH // GROUP):
            best = fold(step * BATCH + part * GROUP, GROUP, best)
        return best

    best = lax.fori_loop(
        0, main // BATCH, batch, jnp.full((queries, LANES), -jnp.inf, jnp.float32))
    lane = lax.broadcasted_iota(jnp.int32, (1, LANES), 1)
    for tile in range(main, rows, 2):
        for h, score in enumerate(scores(tile, 2)):
            if tile + h >= rows - extra:
                last = (tile + h) * LANES + lane
                usable = (me < n - 1) | (last <= rows * LANES - width)
                score = jnp.where(usable, score, -jnp.inf)
            best = jnp.maximum(best, score)
    best = best / (width * t_dev)
    rho = jnp.max(best.T, axis=0, keepdims=True)
    distance = jnp.sqrt(jnp.maximum(2.0 - 2.0 * rho, 0.0))
    profile_ref[...] = distance
    mine[...] = distance
    minima[me] = distance

    def out_copy(step):
        return pltpu.make_async_remote_copy(
            src_ref=mine, dst_ref=minima.at[me],
            send_sem=out_send.at[step], recv_sem=out_recv.at[step],
            device_id=(grp, peer(step)), device_id_type=MESH)

    each(n - 1, lambda step: out_copy(step).start())
    each(n - 1, lambda step: out_copy(step).wait())
    overall_ref[...] = jnp.min(minima[...], axis=0)


def per_device(n, strain, templates):
    width = templates.shape[1]
    held = templates.shape[0]
    queries = n * held
    gathers = held % SUBLANES == 0
    if not gathers:
        templates = lax.all_gather(templates, "seg", axis=0, tiled=True)
    rows = strain.shape[0] // LANES
    extra = width // LANES
    padded = rows + SUBLANES
    dma = pltpu.SemaphoreType.DMA
    vmem = pl.BlockSpec(memory_space=pltpu.VMEM)
    profile, overall = pl.pallas_call(
        functools.partial(kernel, n, width, gathers),
        out_shape=[pltpu.VMEM((1, queries), jnp.float32)] * 2,
        in_specs=[pl.BlockSpec(memory_space=pl.ANY)] * 2,
        out_specs=[vmem] * 2,
        scratch_shapes=[
            pltpu.VMEM((rows, LANES), jnp.bfloat16),
            pltpu.VMEM(templates.shape, jnp.bfloat16),
            pltpu.VMEM((PACKED, LANES), jnp.bfloat16),
            pltpu.VMEM((n, max(held, SUBLANES), width), jnp.bfloat16),
            pltpu.VMEM((SUBLANES, padded * LANES), jnp.float32),
            pltpu.VMEM((LANES, (rows + extra) * LANES), jnp.bfloat16),
            pltpu.VMEM((rows, LANES), jnp.float32),
            pltpu.VMEM((rows, LANES), jnp.float32),
            pltpu.VMEM((n, 1, queries), jnp.float32),
            pltpu.VMEM((1, queries), jnp.float32),
            dma((2,)), dma, dma, dma((n - 1,)), dma((n - 1,)), dma((n - 1,)), dma((n - 1,)),
        ],
        compiler_params=pltpu.CompilerParams(collective_id=0, has_side_effects=True),
    )(strain.reshape(rows, LANES), templates)
    return (profile, overall.reshape(-1))


def solution(mesh):
    in_specs = (P(("grp", "seg")), P("seg", None))
    out_specs = (P(("grp", "seg"), None), P("grp"))
    return jax.shard_map(
        functools.partial(per_device, mesh.shape["seg"]),
        mesh=mesh, in_specs=in_specs, out_specs=out_specs, check_vma=False,
    )
```

```python
import functools

import jax
import jax.numpy as jnp
from jax import lax
from jax.experimental import pallas as pl
from jax.experimental.pallas import tpu as pltpu
from jax.sharding import PartitionSpec as P

EPSILON = 1e-05
LANES = 128
SUBLANES = 8
PACKED = 16
BATCH = 40
GROUP = 4
AHEAD = 3
CHUNK = 10
MESH = pl.DeviceIdType.MESH


def each(count, body):
    if count <= 16:
        for step in range(count):
            body(step)
    else:
        lax.fori_loop(0, count, lambda step, _: (body(step), 0)[1], 0)


def largest_divisor(number, bound):
    return max(d for d in range(1, bound + 1) if number % d == 0)


def largest_multiple(number, of):
    return number // of * of


def window_sums(parts, work, rows, extra):
    source = lax.broadcasted_iota(jnp.int32, (LANES, 2 * LANES), 0)
    place = lax.broadcasted_iota(jnp.int32, (LANES, 2 * LANES), 1)
    from_place = (place < LANES) & (source >= place)
    to_place = (place >= LANES) & (source < place - LANES)
    ones = jnp.where(from_place | to_place, 1.0, 0.0).astype(jnp.bfloat16)
    both = sum(jnp.dot(part, ones, preferred_element_type=jnp.float32) for part in parts)
    first, last = both[:, :LANES], both[:, LANES:]
    work[0] = first + last
    work[1] = last
    total = first[:rows]
    for row in range(1, extra):
        total = total + work[0, pl.ds(row, rows), :]
    return total + work[1, pl.ds(extra, rows), :]


def kernel(n, width, gathers, strain_any, templates_any, profile_ref, overall_ref,
           strain_ref, templates_ref, halo, gathered, longer, work, near, hankel, sums, scales, minima, mine,
           local, halo_send, halo_recv, send, recv, out_send, out_recv):
    me = lax.axis_index("seg")
    grp = lax.axis_index("grp")
    rows = strain_ref.shape[0]
    extra = width // LANES
    tiles = rows + extra
    before = lax.rem(me + n - 1, n)

    def peer(step):
        down = n - 1 - step
        down = jnp.where(down <= me, down - 1, down)
        up = jnp.where(step >= me, step + 1, step)
        return jnp.where(me * 2 < n, down, up)

    fetches = [
        pltpu.make_async_copy(strain_any, strain_ref, local.at[0]),
        pltpu.make_async_copy(templates_any, templates_ref, local.at[1]),
    ]
    for fetch in fetches:
        fetch.start()
    def other(step):
        return jnp.where(step >= me, step + 1, step)

    barrier = pltpu.get_barrier_semaphore()
    each(n - 1, lambda step: pl.semaphore_signal(
        barrier, inc=1, device_id=(grp, peer(step)), device_id_type=MESH))

    def spread(first, count):
        lane = lax.broadcasted_iota(jnp.int32, (count, LANES), 1)
        here = longer[pl.ds(first, count), :]
        below = longer[pl.ds(first + 1, count), :]
        near[pl.ds(first, count), 0, :] = here
        for shift in range(1, PACKED):
            near[pl.ds(first, count), shift, :] = pltpu.roll(
                jnp.where(lane >= shift, here, below), LANES - shift, 1)

    def stagger(first, count):
        span = (count + 1) * LANES
        tiles = near[pl.ds(first, count + 1)].astype(jnp.bfloat16)
        base = jnp.concatenate([tiles[i] for i in range(count + 1)], axis=1)
        start = pl.multiple_of(first * LANES, LANES)
        for group in range(LANES // PACKED):
            turned = base if group == 0 else pltpu.roll(base, span - group * PACKED, 1)
            hankel[pl.ds(group * PACKED, PACKED), pl.ds(start, count * LANES)] = (
                turned[:, : count * LANES])

    for fetch in fetches:
        fetch.wait()
    longer[pl.ds(0, rows), :] = strain_ref[...].astype(jnp.float32)
    longer[pl.ds(rows, PACKED), :] = jnp.zeros((PACKED, LANES), jnp.float32)
    spread(0, rows)
    early = rows - SUBLANES
    chunk = largest_divisor(early, CHUNK)

    def build(step, _):
        stagger(step * chunk, chunk)
        return 0

    steps = early // chunk
    ahead = steps // AHEAD
    lax.fori_loop(0, ahead, build, 0)

    pl.semaphore_wait(barrier, n - 1)

    halo_copy = pltpu.make_async_remote_copy(
        src_ref=strain_ref.at[pl.ds(0, PACKED)], dst_ref=halo,
        send_sem=halo_send, recv_sem=halo_recv, device_id=(grp, before), device_id_type=MESH)
    halo_copy.start()

    def template_copy(step):
        return pltpu.make_async_remote_copy(
            src_ref=templates_ref, dst_ref=gathered.at[me],
            send_sem=send.at[step], recv_sem=recv.at[me],
            device_id=(grp, peer(step)), device_id_type=MESH)

    def template_arrival(sender):
        return pltpu.make_async_remote_copy(
            src_ref=templates_ref, dst_ref=gathered.at[sender],
            send_sem=send.at[0], recv_sem=recv.at[sender],
            device_id=(grp, sender), device_id_type=MESH)

    if gathers:
        each(n - 1, lambda step: template_copy(step).start())
        gathered[me] = templates_ref[...]

    lax.fori_loop(ahead, steps, build, 0)
    halo_copy.wait()
    following = halo[...].astype(jnp.float32)
    following = jnp.where(me == n - 1, jnp.zeros_like(following), following)
    longer[pl.ds(rows, PACKED), :] = following
    spread(early, PACKED)
    stagger(early, tiles - early)

    extended = longer[...]
    square = extended * extended
    high = square.astype(jnp.bfloat16)
    low = (square - high.astype(jnp.float32)).astype(jnp.bfloat16)
    totals = window_sums([extended.astype(jnp.bfloat16)], work.at[0], rows, extra)
    squared = window_sums([high, low], work.at[1], rows, extra)
    win_mean = totals / width
    win_dev = jnp.sqrt(jnp.maximum(squared / width - win_mean * win_mean, 0.0) + EPSILON)
    sums[...] = totals
    scales[...] = 1.0 / win_dev

    def scores(templates, t_wide, tile, count):
        block = jnp.concatenate(
            [hankel[:, pl.ds(pl.multiple_of((tile + c) * LANES, LANES), count * LANES)]
             for c in range(extra)], axis=0)
        products = jnp.dot(templates, block, preferred_element_type=jnp.float32)
        return [
            (products[:, h * LANES : (h + 1) * LANES] - sums[pl.ds(tile + h, 1), :] * t_wide)
            * scales[pl.ds(tile + h, 1), :]
            for h in range(count)
        ]

    main = largest_multiple(rows - extra, BATCH)
    lane = lax.broadcasted_iota(jnp.int32, (1, LANES), 1)

    def largest_rho(floats):
        templates = floats.astype(jnp.bfloat16)
        queries = floats.shape[0]
        t_mean = jnp.mean(floats, axis=1, keepdims=True)
        t_dev = jnp.sqrt(jnp.mean((floats - t_mean) ** 2, axis=1, keepdims=True) + EPSILON)
        t_wide = jnp.broadcast_to(t_mean, (queries, LANES))

        def batch(step, best):
            for part in range(BATCH // GROUP):
                for score in scores(templates, t_wide, step * BATCH + part * GROUP, GROUP):
                    best = jnp.maximum(best, score)
            return best

        best = lax.fori_loop(
            0, main // BATCH, batch, jnp.full((queries, LANES), -jnp.inf, jnp.float32))
        for tile in range(main, rows, 2):
            for h, score in enumerate(scores(templates, t_wide, tile, 2)):
                if tile + h >= rows - extra:
                    last = (tile + h) * LANES + lane
                    usable = (me < n - 1) | (last <= rows * LANES - width)
                    score = jnp.where(usable, score, -jnp.inf)
                best = jnp.maximum(best, score)
        return best / (width * t_dev)

    if gathers:
        each(n - 1, lambda step: template_arrival(other(step)).wait_recv())
        best = largest_rho(gathered[...].astype(jnp.float32).reshape(-1, width))
    else:
        best = largest_rho(templates_ref[...].astype(jnp.float32))
    if gathers:
        each(n - 1, lambda step: template_copy(step).wait_send())
    rho = jnp.max(best.T, axis=0, keepdims=True)
    distance = jnp.sqrt(jnp.maximum(2.0 - 2.0 * rho, 0.0))
    profile_ref[...] = distance
    mine[...] = distance
    minima[me] = distance

    def out_copy(step):
        return pltpu.make_async_remote_copy(
            src_ref=mine, dst_ref=minima.at[me],
            send_sem=out_send.at[step], recv_sem=out_recv.at[me],
            device_id=(grp, peer(step)), device_id_type=MESH)

    def out_arrival(sender):
        return pltpu.make_async_remote_copy(
            src_ref=mine, dst_ref=minima.at[sender],
            send_sem=out_send.at[0], recv_sem=out_recv.at[sender],
            device_id=(grp, sender), device_id_type=MESH)

    each(n - 1, lambda step: out_copy(step).start())
    each(n - 1, lambda step: out_arrival(other(step)).wait_recv())
    each(n - 1, lambda step: out_copy(step).wait_send())
    overall_ref[...] = jnp.min(minima[...], axis=0)


def per_device(n, strain, templates):
    width = templates.shape[1]
    held = templates.shape[0]
    queries = n * held
    gathers = held % SUBLANES == 0
    if not gathers:
        templates = lax.all_gather(templates, "seg", axis=0, tiled=True)
    rows = strain.shape[0] // LANES
    extra = width // LANES
    dma = pltpu.SemaphoreType.DMA
    vmem = pl.BlockSpec(memory_space=pltpu.VMEM)
    profile, overall = pl.pallas_call(
        functools.partial(kernel, n, width, gathers),
        out_shape=[pltpu.VMEM((1, queries), jnp.float32)] * 2,
        in_specs=[pl.BlockSpec(memory_space=pl.ANY)] * 2,
        out_specs=[vmem] * 2,
        scratch_shapes=[
            pltpu.VMEM((rows, LANES), jnp.bfloat16),
            pltpu.VMEM(templates.shape, jnp.bfloat16),
            pltpu.VMEM((PACKED, LANES), jnp.bfloat16),
            pltpu.VMEM((n, max(held, SUBLANES), width), jnp.bfloat16),
            pltpu.VMEM((rows + PACKED, LANES), jnp.float32),
            pltpu.VMEM((2, 2, rows + PACKED, LANES), jnp.float32),
            pltpu.VMEM((rows + SUBLANES, PACKED, LANES), jnp.float32),
            pltpu.VMEM((LANES, (rows + extra) * LANES), jnp.bfloat16),
            pltpu.VMEM((rows, LANES), jnp.float32),
            pltpu.VMEM((rows, LANES), jnp.float32),
            pltpu.VMEM((n, 1, queries), jnp.float32),
            pltpu.VMEM((1, queries), jnp.float32),
            dma((2,)), dma, dma, dma((n - 1,)), dma((n,)), dma((n - 1,)), dma((n,)),
        ],
        compiler_params=pltpu.CompilerParams(collective_id=0, has_side_effects=True),
    )(strain.reshape(rows, LANES), templates)
    return (profile, overall.reshape(-1))


def solution(mesh):
    in_specs = (P(("grp", "seg")), P("seg", None))
    out_specs = (P(("grp", "seg"), None), P("grp"))
    return jax.shard_map(
        functools.partial(per_device, mesh.shape["seg"]),
        mesh=mesh, in_specs=in_specs, out_specs=out_specs, check_vma=False,
    )
```

```python
import functools

import jax
import jax.numpy as jnp
from jax import lax
from jax.experimental import pallas as pl
from jax.experimental.pallas import tpu as pltpu
from jax.sharding import PartitionSpec as P

EPSILON = 1e-05
LANES = 128
SUBLANES = 8
PACKED = 16
BATCH = 120
GROUP = 4
AHEAD = 3
CHUNK = 10
MESH = pl.DeviceIdType.MESH


def each(count, body):
    if count <= 16:
        for step in range(count):
            body(step)
    else:
        lax.fori_loop(0, count, lambda step, _: (body(step), 0)[1], 0)


def largest_divisor(number, bound):
    return max(d for d in range(1, bound + 1) if number % d == 0)


def largest_multiple(number, of):
    return number // of * of


def window_sums(parts, work, rows, extra):
    source = lax.broadcasted_iota(jnp.int32, (LANES, 2 * LANES), 0)
    place = lax.broadcasted_iota(jnp.int32, (LANES, 2 * LANES), 1)
    from_place = (place < LANES) & (source >= place)
    to_place = (place >= LANES) & (source < place - LANES)
    ones = jnp.where(from_place | to_place, 1.0, 0.0).astype(jnp.bfloat16)
    both = sum(jnp.dot(part, ones, preferred_element_type=jnp.float32) for part in parts)
    first, last = both[:, :LANES], both[:, LANES:]
    work[0] = first + last
    work[1] = last
    total = first[:rows]
    for row in range(1, extra):
        total = total + work[0, pl.ds(row, rows), :]
    return total + work[1, pl.ds(extra, rows), :]


def kernel(n, width, gathers, strain_any, templates_any, both_ref,
           strain_ref, templates_ref, halo, gathered, longer, work, near, hankel, sums, scales, minima, mine,
           local, halo_send, halo_recv, send, recv, out_send, out_recv):
    me = lax.axis_index("seg")
    grp = lax.axis_index("grp")
    rows = strain_ref.shape[0]
    extra = width // LANES
    tiles = rows + extra
    before = lax.rem(me + n - 1, n)

    def peer(step):
        down = n - 1 - step
        down = jnp.where(down <= me, down - 1, down)
        up = jnp.where(step >= me, step + 1, step)
        return jnp.where(me * 2 < n, down, up)

    fetches = [
        pltpu.make_async_copy(strain_any, strain_ref, local.at[0]),
        pltpu.make_async_copy(templates_any, templates_ref, local.at[1]),
    ]
    for fetch in fetches:
        fetch.start()
    def other(step):
        return jnp.where(step >= me, step + 1, step)

    barrier = pltpu.get_barrier_semaphore()
    each(n - 1, lambda step: pl.semaphore_signal(
        barrier, inc=1, device_id=(grp, peer(step)), device_id_type=MESH))

    def spread(first, count):
        lane = lax.broadcasted_iota(jnp.int32, (count, LANES), 1)
        here = longer[pl.ds(first, count), :]
        below = longer[pl.ds(first + 1, count), :]
        near[pl.ds(first, count), 0, :] = here
        for shift in range(1, PACKED):
            near[pl.ds(first, count), shift, :] = pltpu.roll(
                jnp.where(lane >= shift, here, below), LANES - shift, 1)

    def stagger(first, count):
        span = (count + 1) * LANES
        tiles = near[pl.ds(first, count + 1)].astype(jnp.bfloat16)
        base = jnp.concatenate([tiles[i] for i in range(count + 1)], axis=1)
        start = pl.multiple_of(first * LANES, LANES)
        for group in range(LANES // PACKED):
            turned = base if group == 0 else pltpu.roll(base, span - group * PACKED, 1)
            hankel[pl.ds(group * PACKED, PACKED), pl.ds(start, count * LANES)] = (
                turned[:, : count * LANES])

    for fetch in fetches:
        fetch.wait()
    longer[pl.ds(0, rows), :] = strain_ref[...].astype(jnp.float32)
    longer[pl.ds(rows, PACKED), :] = jnp.zeros((PACKED, LANES), jnp.float32)
    spread(0, rows)
    early = rows - SUBLANES
    chunk = largest_divisor(early, CHUNK)

    def build(step, _):
        stagger(step * chunk, chunk)
        return 0

    steps = early // chunk
    ahead = steps // AHEAD
    lax.fori_loop(0, ahead, build, 0)

    pl.semaphore_wait(barrier, n - 1)

    halo_copy = pltpu.make_async_remote_copy(
        src_ref=strain_ref.at[pl.ds(0, PACKED)], dst_ref=halo,
        send_sem=halo_send, recv_sem=halo_recv, device_id=(grp, before), device_id_type=MESH)
    halo_copy.start()

    def template_copy(step):
        return pltpu.make_async_remote_copy(
            src_ref=templates_ref, dst_ref=gathered.at[me],
            send_sem=send.at[step], recv_sem=recv.at[me],
            device_id=(grp, peer(step)), device_id_type=MESH)

    def template_arrival(sender):
        return pltpu.make_async_remote_copy(
            src_ref=templates_ref, dst_ref=gathered.at[sender],
            send_sem=send.at[0], recv_sem=recv.at[sender],
            device_id=(grp, sender), device_id_type=MESH)

    if gathers:
        each(n - 1, lambda step: template_copy(step).start())
        gathered[me] = templates_ref[...]

    lax.fori_loop(ahead, steps, build, 0)
    halo_copy.wait()
    following = halo[...].astype(jnp.float32)
    following = jnp.where(me == n - 1, jnp.zeros_like(following), following)
    longer[pl.ds(rows, PACKED), :] = following
    spread(early, PACKED)
    stagger(early, tiles - early)

    extended = longer[...]
    square = extended * extended
    high = square.astype(jnp.bfloat16)
    low = (square - high.astype(jnp.float32)).astype(jnp.bfloat16)
    totals = window_sums([extended.astype(jnp.bfloat16)], work.at[0], rows, extra)
    squared = window_sums([high, low], work.at[1], rows, extra)
    win_mean = totals / width
    win_dev = jnp.sqrt(jnp.maximum(squared / width - win_mean * win_mean, 0.0) + EPSILON)
    sums[...] = totals
    scales[...] = 1.0 / win_dev

    def scores(templates, t_wide, tile, count):
        block = jnp.concatenate(
            [hankel[:, pl.ds(pl.multiple_of((tile + c) * LANES, LANES), count * LANES)]
             for c in range(extra)], axis=0)
        products = jnp.dot(templates, block, preferred_element_type=jnp.float32)
        return [
            (products[:, h * LANES : (h + 1) * LANES] - sums[pl.ds(tile + h, 1), :] * t_wide)
            * scales[pl.ds(tile + h, 1), :]
            for h in range(count)
        ]

    main = largest_multiple(rows - extra, BATCH)
    lane = lax.broadcasted_iota(jnp.int32, (1, LANES), 1)

    def largest_rho(floats):
        templates = floats.astype(jnp.bfloat16)
        queries = floats.shape[0]
        t_mean = jnp.mean(floats, axis=1, keepdims=True)
        t_dev = jnp.sqrt(jnp.mean((floats - t_mean) ** 2, axis=1, keepdims=True) + EPSILON)
        t_wide = jnp.broadcast_to(t_mean, (queries, LANES))

        def batch(step, best):
            for part in range(BATCH // GROUP):
                for score in scores(templates, t_wide, step * BATCH + part * GROUP, GROUP):
                    best = jnp.maximum(best, score)
            return best

        best = lax.fori_loop(
            0, main // BATCH, batch, jnp.full((queries, LANES), -jnp.inf, jnp.float32))
        for tile in range(main, rows, 2):
            for h, score in enumerate(scores(templates, t_wide, tile, 2)):
                if tile + h >= rows - extra:
                    last = (tile + h) * LANES + lane
                    usable = (me < n - 1) | (last <= rows * LANES - width)
                    score = jnp.where(usable, score, -jnp.inf)
                best = jnp.maximum(best, score)
        return best / (width * t_dev)

    if gathers:
        each(n - 1, lambda step: template_arrival(other(step)).wait_recv())
        best = largest_rho(gathered[...].astype(jnp.float32).reshape(-1, width))
    else:
        best = largest_rho(templates_ref[...].astype(jnp.float32))
    if gathers:
        each(n - 1, lambda step: template_copy(step).wait_send())
    rho = jnp.max(best.T, axis=0, keepdims=True)
    distance = jnp.sqrt(jnp.maximum(2.0 - 2.0 * rho, 0.0))
    both_ref[pl.ds(0, 1), :] = distance
    mine[...] = distance
    minima[me] = distance

    def out_copy(step):
        return pltpu.make_async_remote_copy(
            src_ref=mine, dst_ref=minima.at[me],
            send_sem=out_send.at[step], recv_sem=out_recv.at[me],
            device_id=(grp, peer(step)), device_id_type=MESH)

    def out_arrival(sender):
        return pltpu.make_async_remote_copy(
            src_ref=mine, dst_ref=minima.at[sender],
            send_sem=out_send.at[0], recv_sem=out_recv.at[sender],
            device_id=(grp, sender), device_id_type=MESH)

    each(n - 1, lambda step: out_copy(step).start())
    each(n - 1, lambda step: out_arrival(other(step)).wait_recv())
    each(n - 1, lambda step: out_copy(step).wait_send())
    both_ref[pl.ds(1, 1), :] = jnp.min(minima[...], axis=0)


def per_device(n, strain, templates):
    width = templates.shape[1]
    held = templates.shape[0]
    queries = n * held
    gathers = held % SUBLANES == 0
    if not gathers:
        templates = lax.all_gather(templates, "seg", axis=0, tiled=True)
    rows = strain.shape[0] // LANES
    extra = width // LANES
    dma = pltpu.SemaphoreType.DMA
    vmem = pl.BlockSpec(memory_space=pltpu.VMEM)
    both = pl.pallas_call(
        functools.partial(kernel, n, width, gathers),
        out_shape=pltpu.VMEM((2, queries), jnp.float32),
        in_specs=[pl.BlockSpec(memory_space=pl.ANY)] * 2,
        out_specs=vmem,
        scratch_shapes=[
            pltpu.VMEM((rows, LANES), jnp.bfloat16),
            pltpu.VMEM(templates.shape, jnp.bfloat16),
            pltpu.VMEM((PACKED, LANES), jnp.bfloat16),
            pltpu.VMEM((n, max(held, SUBLANES), width), jnp.bfloat16),
            pltpu.VMEM((rows + PACKED, LANES), jnp.float32),
            pltpu.VMEM((2, 2, rows + PACKED, LANES), jnp.float32),
            pltpu.VMEM((rows + SUBLANES, PACKED, LANES), jnp.float32),
            pltpu.VMEM((LANES, (rows + extra) * LANES), jnp.bfloat16),
            pltpu.VMEM((rows, LANES), jnp.float32),
            pltpu.VMEM((rows, LANES), jnp.float32),
            pltpu.VMEM((n, 1, queries), jnp.float32),
            pltpu.VMEM((1, queries), jnp.float32),
            dma((2,)), dma, dma, dma((n - 1,)), dma((n,)), dma((n - 1,)), dma((n,)),
        ],
        compiler_params=pltpu.CompilerParams(collective_id=0, has_side_effects=True),
    )(strain.reshape(rows, LANES), templates)
    return (both[:1], both[1])


def solution(mesh):
    in_specs = (P(("grp", "seg")), P("seg", None))
    out_specs = (P(("grp", "seg"), None), P("grp"))
    return jax.shard_map(
        functools.partial(per_device, mesh.shape["seg"]),
        mesh=mesh, in_specs=in_specs, out_specs=out_specs, check_vma=False,
    )
```
